1024 devices in a mesh: dp: 32 (over z, core), expert: 32 (over y, x).
Axes of the slice: x: 4, y: 8, z: 16, core: 2. Of those that a mesh axis runs over, the one named last changes fastest.
Arguments:
- tokens: bfloat16 [32768, 2048], P(('dp', 'expert')), may hold values from -6 to 6
- routes: int32 [32768, 6], P(('dp', 'expert')), may hold values from 0 to 31, all different within a row; in each aligned block of 32 rows (0 to 31, 32 to 63, ...) at most 7 rows name the same one
- weights_fwd: float32 [32768, 6], P(('dp', 'expert')), may hold values from 0.05 to 0.45
- cotangent: bfloat16 [32768, 2048], P(('dp', 'expert')), may hold values from -6 to 6
- routes_back: int32 [32768, 6], P(('dp', 'expert')), may hold values from 0 to 31, all different within a row; in each aligned block of 32 rows (0 to 31, 32 to 63, ...) at most 7 rows name the same one
- weights_back: float32 [32768, 6], P(('dp', 'expert')), may hold values from 0.05 to 0.45
- saved_gate: bfloat16 [32, 32, 32, 7, 704], P('dp', None, 'expert'), may hold values from -5 to 5
- saved_up: bfloat16 [32, 32, 32, 7, 704], P('dp', None, 'expert'), may hold values from -5 to 5
- w_gate: bfloat16 [32, 2048, 704], P('expert'), may hold values from -0.125 to 0.125
- w_up: bfloat16 [32, 2048, 704], P('expert'), may hold values from -0.125 to 0.125
- w_down: bfloat16 [32, 704, 2048], P('expert'), may hold values from -0.21875 to 0.21875
Outputs:
- mixed: bfloat16 [32768, 2048], P(('dp', 'expert'))
- input_grad: bfloat16 [32768, 2048], P(('dp', 'expert'))
- weight_grad: float32 [32768, 6], P(('dp', 'expert'))
The draws below stay inside these ranges and needn't reach their ends.
Inputs may be any that keep to these rules, and one draw needn't show every extreme that they name: `routes`: each row names 6 different experts; among the 32 rows of one device no expert is named more than 7 times, and in every draw some expert is named exactly 7 times by one device. `routes_back`: each row names 6 different experts; among the 32 rows of one device no expert is named more than 7 times, and in every draw some expert is named exactly 7 times by one device.
All inputs are finite; a program needn't handle non-finite values.
Results may differ from the reference program's by a relative error of at most 0.0057.
Values may be sent and summed in bfloat16 or wider, within the bound.
A program may use at most 64 MiB of HBM per device.

```python
import math
import jax
import jax.numpy as jnp
import numpy as np

D = 2048
FF = 704
EXPERTS = 32
TOPK = 6
TOK_DEV = 32
CAP = 7
TOKENS = 32768
N_DP = 32
N_EXPERT = 32
DEVICES = 1024


def level_of(own_key, dims, split, low, high):
    def one(position, parts):
        heights = jax.random.uniform(jax.random.fold_in(jax.random.fold_in(own_key, 6), position), (parts,), jnp.float32, low / len(split), high / len(split))
        return jnp.repeat(jnp.exp(heights), dims[position] // parts).reshape((-1,) + (1,) * (len(dims) - position - 1))

    gain = one(*split[0])
    for cut in split[1:]:
        gain = gain * one(*cut)
    return gain


def deal_out(rng, own, number, rows, amount, top, limit, skew):
    order = jax.random.permutation(rng, amount)
    packed, common = portions_of(amount, rows * top, limit, skew, True), portions_of(amount, rows * top, limit, skew, False)
    places = jnp.arange(amount)

    def named(lengths, rotation):
        used = int((lengths > 0).sum())
        fixed = max(1, used // 4)
        shifted = fixed + (places - fixed + rotation * (used - fixed)) % max(1, amount - fixed)
        return jnp.zeros((amount,), jnp.int32).at[order[jnp.where(places < fixed, places, shifted)]].set(jnp.asarray(lengths, jnp.int32))

    lengths = jnp.where(number % 4 == 0, named(packed, number // 4), named(common, number - number // 4 - 1))
    mixed = jax.random.permutation(jax.random.fold_in(own, 3), amount)
    donor, sink = mixed[0:amount // 2 * 2:2], mixed[1:amount // 2 * 2:2]
    slack = jnp.minimum(lengths[donor] - 1, limit - lengths[sink]) // 2
    slack = jnp.where((donor == order[0]) | (sink == order[0]) | (lengths[sink] == 0), 0, jnp.maximum(slack, 0))
    shifted = jax.random.randint(jax.random.fold_in(own, 4), (amount // 2,), 0, 1 << 20) % (slack + 1)
    lengths = lengths.at[donor].add(-shifted).at[sink].add(shifted)
    items = jnp.searchsorted(jnp.cumsum(lengths), jnp.arange(rows * top), side="right").astype(jnp.int32)
    table = items.reshape(top, rows).T
    table = table[jax.random.permutation(jax.random.fold_in(own, 1), rows)]
    rotation = jax.random.randint(jax.random.fold_in(own, 2), (rows, 1), 0, top)
    return jnp.take_along_axis(table, (jnp.arange(top)[None, :] + rotation) % top, axis=1)


def portions_of(amount, total, limit, lean, full):
    loads = [(1 << 20) // math.isqrt(standing ** lean) + 1 for standing in range(1, amount + 1)]
    largest = limit if full else min(limit, max(-(-total // amount), total * loads[0] // sum(loads)))
    least = 1 if total - largest >= amount - 1 else 0
    holding, rest = [largest] + [least] * (amount - 1), total - largest - least * (amount - 1)
    while rest > 0:
        free = [i for i in range(1, amount) if holding[i] < largest] or [i for i in range(1, amount) if holding[i] < limit]
        pool, budget = sum([loads[i] for i in free]), rest
        for i in free:
            addition = min(limit - holding[i], max(1, budget * loads[i] // pool), rest)
            holding[i] = holding[i] + addition
            rest = rest - addition
    return np.array(holding)


def normal_values(own_key, extent, scale, most, pieces=(), kind=jnp.bfloat16):
    factor_of = level_of(own_key, extent, pieces, -0.22, 0.18) if pieces else 1.0
    drawn = jax.random.normal(own_key, extent, jnp.float32) * scale * factor_of
    return jnp.minimum(jnp.maximum(drawn, -most), most).astype(kind)


def setup_inputs(seed: int = 0) -> dict:
    arg_keys = jax.random.split(jax.random.key(seed), 12)
    tokens = normal_values(arg_keys[0], (TOKENS, D), 1.0, 6.0, ((0, 1024),))
    routes_keys = jax.random.split(jax.random.fold_in(arg_keys[1], 1), TOKENS // TOK_DEV)
    routes_turns = jax.random.permutation(jax.random.fold_in(arg_keys[1], 3), TOKENS // TOK_DEV)
    routes = jax.vmap(lambda own, number: deal_out(jax.random.fold_in(arg_keys[1], 2), own, number, TOK_DEV, EXPERTS, TOPK, CAP, 2))(routes_keys, routes_turns).reshape((TOKENS, TOPK))
    weights_fwd = jnp.clip(0.05 + 0.39999999 * jax.random.uniform(arg_keys[2], (TOKENS, TOPK), jnp.float32) ** level_of(arg_keys[2], (TOKENS, TOPK), ((0, 1024),), -0.2, 0.2), 0.05, 0.45)
    cotangent = normal_values(arg_keys[3], (TOKENS, D), 1.0, 6.0, ((0, 1024),))
    routes_back_keys = jax.random.split(jax.random.fold_in(arg_keys[4], 1), TOKENS // TOK_DEV)
    routes_back_turns = jax.random.permutation(jax.random.fold_in(arg_keys[4], 3), TOKENS // TOK_DEV)
    routes_back = jax.vmap(lambda own, number: deal_out(jax.random.fold_in(arg_keys[4], 2), own, number, TOK_DEV, EXPERTS, TOPK, CAP, 2))(routes_back_keys, routes_back_turns).reshape((TOKENS, TOPK))
    weights_back = jnp.clip(0.05 + 0.39999999 * jax.random.uniform(arg_keys[5], (TOKENS, TOPK), jnp.float32) ** level_of(arg_keys[5], (TOKENS, TOPK), ((0, 1024),), -0.2, 0.2), 0.05, 0.45)
    saved_gate = normal_values(arg_keys[6], (N_DP, N_EXPERT, EXPERTS, CAP, FF), 1.0, 5.0, ((0, 32), (2, 32)))
    saved_up = normal_values(arg_keys[7], (N_DP, N_EXPERT, EXPERTS, CAP, FF), 1.0, 5.0, ((0, 32), (2, 32)))
    w_gate = normal_values(arg_keys[8], (EXPERTS, D, FF), D ** -0.5, 0.125, ((0, 32),))
    w_up = normal_values(arg_keys[9], (EXPERTS, D, FF), D ** -0.5, 0.125, ((0, 32),))
    w_down = normal_values(arg_keys[10], (EXPERTS, FF, D), FF ** -0.5, 0.21875, ((0, 32),))
    return {"tokens": tokens, "routes": routes, "weights_fwd": weights_fwd, "cotangent": cotangent, "routes_back": routes_back, "weights_back": weights_back, "saved_gate": saved_gate, "saved_up": saved_up, "w_gate": w_gate, "w_up": w_up, "w_down": w_down}


def slot_places(ids):
    count, top = ids.shape
    flat = ids.reshape(-1)
    onehot = (flat[:, None] == jnp.arange(EXPERTS, dtype=jnp.int32)[None, :]).astype(jnp.int32)
    before = jnp.cumsum(onehot, axis=0) - onehot
    slot = jnp.sum(before * onehot, axis=1)
    return (flat * CAP + slot).reshape(count, top).astype(jnp.int32)


def dispatch(places, rows):
    count, top = places.shape
    table = (places.reshape(-1)[None, :] == jnp.arange(EXPERTS * CAP, dtype=jnp.int32)[:, None])
    table = jnp.sum(table.reshape(EXPERTS * CAP, count, top).astype(jnp.float32), axis=2)
    return jnp.dot(table, rows.astype(jnp.float32), preferred_element_type=jnp.float32).astype(jnp.bfloat16)


def combine(flat_out, places, factors):
    picked = flat_out[places].astype(jnp.float32)
    return jnp.sum(factors[:, :, None] * picked, axis=1)


def reference(tokens, routes, weights_fwd, cotangent, routes_back, weights_back, saved_gate, saved_up, w_gate, w_up, w_down):
    blocks = DEVICES
    wg = w_gate.astype(jnp.float32)
    wu = w_up.astype(jnp.float32)
    wd = w_down.astype(jnp.float32)
    places = jax.vmap(slot_places)(routes.reshape(blocks, TOK_DEV, TOPK))
    places_back = jax.vmap(slot_places)(routes_back.reshape(blocks, TOK_DEV, TOPK))
    buffer = jax.vmap(dispatch)(places, tokens.reshape(blocks, TOK_DEV, D)).reshape(blocks, EXPERTS, CAP, D)
    grad_buffer = jax.vmap(dispatch)(places_back, cotangent.reshape(blocks, TOK_DEV, D)).reshape(blocks, EXPERTS, CAP, D)
    xb = buffer.astype(jnp.float32)
    gate = jnp.einsum('becd,edf->becf', xb, wg)
    up = jnp.einsum('becd,edf->becf', xb, wu)
    hidden = (jax.nn.silu(gate) * up).astype(jnp.bfloat16)
    expert_out = jnp.einsum('becf,efd->becd', hidden.astype(jnp.float32), wd).astype(jnp.bfloat16)
    mixed = jax.vmap(combine)(expert_out.reshape(blocks, EXPERTS * CAP, D), places, weights_fwd.reshape(blocks, TOK_DEV, TOPK))
    mixed = mixed.reshape(TOKENS, D).astype(jnp.bfloat16)
    act_in = saved_gate.reshape(blocks, EXPERTS, CAP, FF).astype(jnp.float32)
    up_in = saved_up.reshape(blocks, EXPERTS, CAP, FF).astype(jnp.float32)
    grad_hidden = jnp.einsum('becd,efd->becf', grad_buffer.astype(jnp.float32), wd)
    sig = jax.nn.sigmoid(act_in)
    silu_in = act_in * sig
    score = jnp.sum(silu_in * up_in * grad_hidden, axis=3)
    grad_gate = (grad_hidden * up_in * sig * (1.0 + act_in * (1.0 - sig))).astype(jnp.bfloat16)
    grad_up = (grad_hidden * silu_in).astype(jnp.bfloat16)
    expert_grad = jnp.einsum('becf,edf->becd', grad_gate.astype(jnp.float32), wg) + jnp.einsum('becf,edf->becd', grad_up.astype(jnp.float32), wu)
    expert_grad = expert_grad.astype(jnp.bfloat16)
    input_grad = jax.vmap(combine)(expert_grad.reshape(blocks, EXPERTS * CAP, D), places_back, weights_back.reshape(blocks, TOK_DEV, TOPK))
    input_grad = input_grad.reshape(TOKENS, D).astype(jnp.bfloat16)
    weight_grad = jax.vmap(lambda flat, pl: flat[pl])(score.reshape(blocks, EXPERTS * CAP), places_back).reshape(TOKENS, TOPK)
    return mixed, input_grad, weight_grad
```

```python
import jax
import jax.numpy as jnp
from jax import lax
from jax.experimental import pallas as pl
from jax.experimental.pallas import tpu as pltpu
from jax.sharding import PartitionSpec as P

NX, NY = 4, 8
TOPK = 6
CAP = 7
TOK = 32
NC = 4
PAD = 64
ROWS = CAP * NY
SLOTS = NX * PAD
F32, BF16 = jnp.float32, jnp.bfloat16
DOWN, UP = 0, 1


def nn(a, b):
    return jnp.dot(a, b, preferred_element_type=F32)


def nt(a, b):
    return lax.dot_general(a, b, (((1,), (1,)), ((), ())), preferred_element_type=F32)


def iota(shape, axis):
    return lax.broadcasted_iota(jnp.int32, shape, axis)


def wrap(v, n):
    return jnp.where(v >= n, v - n, v)


def halves(v):
    top = v.astype(BF16)
    return top, (v - top.astype(F32)).astype(BF16)


def hops(c, way):
    return 4 if c % 2 == way else 3


def kernel(
    tok_hbm, cot_hbm, meta_ref, sg_hbm, su_hbm, wg_hbm, wu_hbm, wd_hbm,
    mixed_hbm, grad_hbm, wgrad_ref,
    wg, wu, wd, sg, su, G, XS, X, OUT, OR, PS, R, SB, OB, MS, MR, SCS, SCR, SYS, SYR,
    S, CH, CL, MT, acc_a, acc_b, co_g, co_u, co_s,
    ag_s, ag_r, xd_s, xd_r, xr_s, xr_r, rs_s, rs_r, mt_s, mt_r, sc_s, sc_r, sy_s, sy_r, ld, own, outs,
):
    me = lax.axis_index("expert")
    y, x = lax.div(me, NX), lax.rem(me, NX)
    depth = tok_hbm.shape[1]
    W = depth // NC

    def at_y(o):
        return {"expert": lax.rem(y + o, NY) * NX + x}

    def at_x(p):
        return {"expert": y * NX + lax.rem(x + p, NX)}

    def cols(c):
        return pl.ds(c * W, W)

    ins = (tok_hbm, cot_hbm)
    results = (mixed_hbm, grad_hbm)
    remote = pltpu.make_async_remote_copy

    def gather_hop(m, c, way, h):
        a, b = (h, h + 1) if way == DOWN else ((NY - h) % NY, NY - 1 - h)
        src = ins[m].at[:, cols(c)] if h == 0 else G.at[m, c, a]
        return remote(src, G.at[m, c, b], ag_s.at[m, c, way, h], ag_r.at[m, c, way, h],
                      device_id=at_y(NY - 1 if way == DOWN else 1))

    def to_expert(m, c, p):
        q = NX - p
        return remote(XS.at[m, c, p - 1, pl.ds(0, ROWS)], X.at[m, c, q, pl.ds(0, ROWS)],
                      xd_s.at[m, c, p - 1], xd_r.at[m, c, q - 1], device_id=at_x(p))

    def from_expert(m, c, q):
        p = NX - q
        return remote(OUT.at[m, c, q - 1, pl.ds(0, ROWS)], OR.at[m, c, p, pl.ds(0, ROWS)],
                      xr_s.at[m, c, q - 1], xr_r.at[m, c, p - 1], device_id=at_x(q))

    def sum_hop(m, c, way, k):
        return remote(SB.at[m, c, way, k - 1], R.at[m, c, way, k - 1], rs_s.at[m, c, way, k - 1],
                      rs_r.at[m, c, way, k - 1], device_id=at_y(NY - 1 if way == DOWN else 1))

    def meta_to(o):
        return remote(MS.at[o], MR.at[NY - o], mt_s.at[o - 1], mt_r.at[NY - o - 1], device_id=at_y(o))

    def score_to(q):
        return remote(SCS, SCR.at[NX - q - 1], sc_s.at[q - 1], sc_r.at[NX - q - 1], device_id=at_x(q))

    def score_back(o):
        return remote(SYS.at[o], SYR.at[NY - o], sy_s.at[o - 1], sy_r.at[NY - o - 1], device_id=at_y(o))

    def own_rows(m, c):
        return pltpu.make_async_copy(ins[m].at[:, cols(c)], G.at[m, c, 0], own.at[m, c])

    def result(m, c):
        return pltpu.make_async_copy(OB.at[m, c], results[m].at[:, cols(c)], outs.at[m, c])

    barrier = pltpu.get_barrier_semaphore()
    for o in range(1, NY):
        pl.semaphore_signal(barrier, inc=1, device_id=at_y(o))
    for p in range(1, NX):
        pl.semaphore_signal(barrier, inc=1, device_id=at_x(p))
    loads = [
        pltpu.make_async_copy(a, b, ld.at[i])
        for i, (a, b) in enumerate(((wg_hbm, wg), (wu_hbm, wu), (wd_hbm, wd), (sg_hbm, sg), (su_hbm, su)))
    ]
    for m in range(2):
        for c in range(NC):
            own_rows(m, c).start()
    for load in loads:
        load.start()

    lane = iota((NY, 128), 1)
    named = (wrap(y + iota((NY, 128), 0), NY) * NX + wrap(x + lane // TOK, NX)).astype(F32)
    before = (iota((128, 128), 0) // TOK == iota((128, 128), 1) // TOK) & (iota((128, 128), 0) < iota((128, 128), 1))
    before = before.astype(F32).astype(BF16)
    table = []
    for m in range(2):
        has, weight = jnp.zeros((NY, 128), F32), jnp.zeros((NY, 128), F32)
        for k in range(TOPK):
            hit = named == meta_ref[m, 0, k:k + 1, :]
            has = has + jnp.where(hit, 1.0, 0.0)
            weight = weight + jnp.where(hit, meta_ref[m, 1, k:k + 1, :], 0.0)
        slot = nn(has.astype(BF16), before)
        table += [jnp.where(has > 0, slot, -1.0), weight]
    for o in range(NY):
        for i, rows in enumerate(table):
            MS[o, i:i + 1, :] = rows[o:o + 1, :]
        MS[o, 4:8, :] = jnp.zeros((4, 128), F32)
    MR[0] = MS[0]

    for m in range(2):
        for c in range(NC):
            for p in range(1, NX):
                X[m, c, p, ROWS:PAD, :] = jnp.zeros((PAD - ROWS, W), BF16)
                OR[m, c, p, ROWS:PAD, :] = jnp.zeros((PAD - ROWS, W), BF16)

    pl.semaphore_wait(barrier, NY - 1 + NX - 1)

    def start_own(m):
        for c in range(NC):
            for way in (DOWN, UP):
                gather_hop(m, c, way, 0).start()

    def pass_on(m, h):
        for c in range(NC):
            for way in (DOWN, UP):
                if h < hops(c, way):
                    gather_hop(m, c, way, h - 1).wait_recv()
                    gather_hop(m, c, way, h).start()

    start_own(0)
    for o in range(1, NY):
        meta_to(o).start()

    loads[3].wait()
    loads[4].wait()
    r, cj = iota((SLOTS, CAP * TOK), 0), iota((SLOTS, CAP * TOK), 1)
    source = wrap(y + r % NY, NY) * NX + wrap(x + r // PAD, NX)
    order = ((r % PAD) // NY == cj // 32) & (source == cj % 32)
    order = order.astype(F32).astype(BF16)
    ff = wd_hbm.shape[0]
    a = nn(order, sg[...].reshape(CAP * 32, ff))
    u = nn(order, su[...].reshape(CAP * 32, ff))
    sig = 1.0 / (1.0 + jnp.exp(-a))
    act = a * sig
    co_g[...] = u * sig * (1.0 + a * (1.0 - sig))
    co_u[...] = act
    co_s[...] = act * u

    pass_on(0, 1)
    pass_on(0, 2)
    start_own(1)
    pass_on(0, 3)

    for o in range(1, NY):
        meta_to(o).wait_recv()
    r128, l128 = iota((SLOTS, 128), 0), iota((SLOTS, 128), 1)
    place = l128 // TOK == r128 // PAD
    fold = (r128 % TOK == l128 % TOK).astype(F32).astype(BF16)
    block = iota((SLOTS, SLOTS), 0) % NY == iota((SLOTS, SLOTS), 1) // TOK
    back = iota((SLOTS, SLOTS), 1) % NY == iota((SLOTS, SLOTS), 0) // TOK
    for m in range(2):
        slots = jnp.concatenate([MR[o, 2 * m:2 * m + 1, :] for o in range(NY)], axis=0)
        weights = jnp.concatenate([MR[o, 2 * m + 1:2 * m + 2, :] for o in range(NY)], axis=0)
        slots = jnp.broadcast_to(slots[None], (SLOTS // NY, NY, 128)).reshape(SLOTS, 128)
        weights = jnp.broadcast_to(weights[None], (SLOTS // NY, NY, 128)).reshape(SLOTS, 128)
        hit = (slots == ((r128 % PAD) // NY).astype(F32)) & place
        match = jnp.where(hit, 1.0, 0.0).astype(BF16)
        top, rest = halves(jnp.where(hit, weights, 0.0))
        S[m] = jnp.where(block, nt(match, fold), 0.0).astype(BF16)
        CH[m] = jnp.where(back, nt(fold, top), 0.0).astype(BF16)
        CL[m] = jnp.where(back, nt(fold, rest), 0.0).astype(BF16)
        if m == 1:
            MT[...] = match

    def send_slots(m):
        for c in range(NC):
            own_rows(m, c).wait()
            for way in (DOWN, UP):
                gather_hop(m, c, way, hops(c, way) - 1).wait_recv()
            rows = nn(S[m], G[m, c].reshape(NY * TOK, W)).astype(BF16).reshape(NX, PAD, W)
            for p in range(1, NX):
                XS[m, c, p - 1] = rows[p]
            for p in (2, 1, 3):
                to_expert(m, c, p).start()
            X[m, c, 0] = rows[0]

    def arrived(m, c):
        for p in range(1, NX):
            to_expert(m, c, p).wait_recv()
        return X[m, c].reshape(SLOTS, W)

    def give_back(m, c, value):
        value = value.astype(BF16).reshape(NX, PAD, W)
        for q in range(1, NX):
            OUT[m, c, q - 1] = value[q]
        for q in (2, 1, 3):
            from_expert(m, c, q).start()
        OR[m, c, 0] = value[0]

    send_slots(0)
    pass_on(1, 1)
    pass_on(1, 2)
    pass_on(1, 3)
    send_slots(1)

    for load in loads[:3]:
        load.wait()
    for c in range(NC):
        rows = arrived(0, c)
        g, v = nt(rows, wg[:, cols(c)]), nt(rows, wu[:, cols(c)])
        acc_a[...] = g if c == 0 else acc_a[...] + g
        acc_b[...] = v if c == 0 else acc_b[...] + v
    g = acc_a[...]
    hidden = (g / (1.0 + jnp.exp(-g)) * acc_b[...]).astype(BF16)
    for c in range(NC):
        give_back(0, c, nn(hidden, wd[:, cols(c)]))

    for c in range(NC):
        part = nt(arrived(1, c), wd[:, cols(c)])
        acc_a[...] = part if c == 0 else acc_a[...] + part
    gh = acc_a[...]
    gg, gu = (gh * co_g[...]).astype(BF16), (gh * co_u[...]).astype(BF16)
    top, rest = halves(gh * co_s[...])
    for c in range(NC):
        give_back(1, c, nn(gg, wg[:, cols(c)]) + nn(gu, wu[:, cols(c)]))
    ones = jnp.ones((NY, ff), BF16)
    score = nt(ones, top) + nt(ones, rest)
    SCS[...] = score
    for q in range(1, NX):
        score_to(q).start()

    def send_sum(m, c, way, k):
        o = NY - k if way == DOWN else k
        value = PS[m, c, o]
        if k < hops(c, way):
            sum_hop(m, c, way, k + 1).wait_recv()
            value = value + R[m, c, way, k].astype(F32)
        SB[m, c, way, k - 1] = value.astype(BF16)
        sum_hop(m, c, way, k).start()

    def stage(m, c, s):
        if s == 0:
            for p in range(1, NX):
                from_expert(m, c, NX - p).wait_recv()
            rows = OR[m, c].reshape(SLOTS, W)
            PS[m, c] = (nn(CH[m], rows) + nn(CL[m], rows)).reshape(NY, TOK, W)
        for way in (DOWN, UP):
            if hops(c, way) > s:
                send_sum(m, c, way, hops(c, way) - s)
        if s == 4:
            for way in (DOWN, UP):
                sum_hop(m, c, way, 1).wait_recv()
            OB[m, c] = (PS[m, c, 0] + R[m, c, DOWN, 0].astype(F32) + R[m, c, UP, 0].astype(F32)).astype(BF16)
            result(m, c).start()

    def scores_on():
        mine = iota((NY, PAD), 1) % NY == iota((NY, PAD), 0)
        total = jnp.zeros((NY, 128), F32)
        for p in range(NX):
            if p:
                score_to(NX - p).wait_recv()
            q = (NX - p) % NX
            row = SCS[:, q * PAD:(q + 1) * PAD] if p == 0 else SCR[p - 1, :, q * PAD:(q + 1) * PAD]
            rest = jnp.where(mine, row, 0.0)
            for _ in range(3):
                top, rest2 = rest.astype(BF16), rest - rest.astype(BF16).astype(F32)
                total = total + nn(top, MT[p * PAD:(p + 1) * PAD, :])
                rest = rest2
        for o in range(NY):
            SYS[o] = jnp.broadcast_to(total[o:o + 1, :], (8, 128))
        for o in range(1, NY):
            score_back(o).start()
        SYR[0] = SYS[0]

    def scores_home():
        for o in range(1, NY):
            score_back(o).wait_recv()
        rows = jnp.concatenate([SYR[o, 0:1, :] for o in range(NY)], axis=0)
        for k in range(8):
            v = jnp.sum(jnp.where(named == meta_ref[1, 0, k:k + 1, :], rows, 0.0), axis=0, keepdims=True)
            v = jnp.broadcast_to(v, (8, 128))
            v = v + pltpu.roll(v, 64, 1)
            v = v + pltpu.roll(v, 32, 1)
            wgrad_ref[k:k + 1, :] = v[0:1, :]

    items = [(m, c) for m in range(2) for c in range(NC)]
    for wave in range(len(items) + 4):
        for s in range(4, -1, -1):
            if 0 <= wave - s < len(items):
                stage(*items[wave - s], s)
        if wave == NC:
            scores_on()
        if wave == NC + 4:
            scores_home()

    for m, c in items:
        for way in (DOWN, UP):
            for h in range(hops(c, way)):
                gather_hop(m, c, way, h).wait_send()
                sum_hop(m, c, way, h + 1).wait_send()
        for p in range(1, NX):
            to_expert(m, c, p).wait_send()
            from_expert(m, c, p).wait_send()
    for o in range(1, NY):
        meta_to(o).wait_send()
        score_back(o).wait_send()
    for q in range(1, NX):
        score_to(q).wait_send()
    for m, c in items:
        result(m, c).wait()


def window(tokens, cotangent, meta, saved_gate, saved_up, w_gate, w_up, w_down):
    depth, ff = tokens.shape[1], w_down.shape[0]
    W = depth // NC
    whole = pl.BlockSpec(memory_space=pl.ANY)
    vmem = pl.BlockSpec(memory_space=pltpu.VMEM)
    dma = pltpu.SemaphoreType.DMA
    return pl.pallas_call(
        kernel,
        name="window",
        out_shape=(
            jax.ShapeDtypeStruct((TOK, depth), BF16),
            jax.ShapeDtypeStruct((TOK, depth), BF16),
            jax.ShapeDtypeStruct((8, 128), F32),
        ),
        in_specs=[whole, whole, vmem, whole, whole, whole, whole, whole],
        out_specs=(whole, whole, vmem),
        scratch_shapes=[
            pltpu.VMEM((ff, depth), BF16),
            pltpu.VMEM((ff, depth), BF16),
            pltpu.VMEM((ff, depth), BF16),
            pltpu.VMEM((CAP, 32, ff), BF16),
            pltpu.VMEM((CAP, 32, ff), BF16),
            pltpu.VMEM((2, NC, NY, TOK, W), BF16),
            pltpu.VMEM((2, NC, NX - 1, PAD, W), BF16),
            pltpu.VMEM((2, NC, NX, PAD, W), BF16),
            pltpu.VMEM((2, NC, NX - 1, PAD, W), BF16),
            pltpu.VMEM((2, NC, NX, PAD, W), BF16),
            pltpu.VMEM((2, NC, NY, TOK, W), F32),
            pltpu.VMEM((2, NC, 2, 4, TOK, W), BF16),
            pltpu.VMEM((2, NC, 2, 4, TOK, W), BF16),
            pltpu.VMEM((2, NC, TOK, W), BF16),
            pltpu.VMEM((NY, 8, 128), F32),
            pltpu.VMEM((NY, 8, 128), F32),
            pltpu.VMEM((8, SLOTS), F32),
            pltpu.VMEM((NX - 1, 8, SLOTS), F32),
            pltpu.VMEM((NY, 8, 128), F32),
            pltpu.VMEM((NY, 8, 128), F32),
            pltpu.VMEM((2, SLOTS, SLOTS), BF16),
            pltpu.VMEM((2, SLOTS, SLOTS), BF16),
            pltpu.VMEM((2, SLOTS, SLOTS), BF16),
            pltpu.VMEM((SLOTS, 128), BF16),
            pltpu.VMEM((SLOTS, ff), F32),
            pltpu.VMEM((SLOTS, ff), F32),
            pltpu.VMEM((SLOTS, ff), F32),
            pltpu.VMEM((SLOTS, ff), F32),
            pltpu.VMEM((SLOTS, ff), F32),
            dma((2, NC, 2, 4)), dma((2, NC, 2, 4)),
            dma((2, NC, 3)), dma((2, NC, 3)),
            dma((2, NC, 3)), dma((2, NC, 3)),
            dma((2, NC, 2, 4)), dma((2, NC, 2, 4)),
            dma((7,)), dma((7,)), dma((3,)), dma((3,)), dma((7,)), dma((7,)),
            dma((5,)), dma((2, NC)), dma((2, NC)),
        ],
        compiler_params=pltpu.CompilerParams(
            collective_id=0, has_side_effects=True, vmem_limit_bytes=60 * 1024 * 1024
        ),
    )(tokens, cotangent, meta, saved_gate, saved_up, w_gate, w_up, w_down)


def lanes(routes, weights):
    ids = jnp.pad(routes.T.astype(F32), ((0, 8 - TOPK), (0, 0)), constant_values=-1.0)
    factors = jnp.pad(weights.T, ((0, 8 - TOPK), (0, 0)))
    return jnp.tile(jnp.stack([ids, factors]), (1, 1, 128 // TOK))


def body(
    tokens, routes, weights_fwd, cotangent, routes_back, weights_back, saved_gate, saved_up, w_gate, w_up, w_down
):
    meta = jnp.stack([lanes(routes, weights_fwd), lanes(routes_back, weights_back)])
    mixed, input_grad, wgrad = window(
        tokens, cotangent, meta,
        saved_gate[0, :, 0].transpose(1, 0, 2), saved_up[0, :, 0].transpose(1, 0, 2),
        w_gate[0].T, w_up[0].T, w_down[0],
    )
    return mixed, input_grad, wgrad[:TOPK, :TOK].T


def solution(mesh):
    rows = P(("dp", "expert"), None)
    saved = P("dp", None, "expert", None, None)
    weight = P("expert", None, None)
    return jax.shard_map(
        body,
        mesh=mesh,
        in_specs=(rows,) * 6 + (saved, saved, weight, weight, weight),
        out_specs=(rows, rows, rows),
        check_vma=False,
    )
```

```python
import jax
import jax.numpy as jnp
from jax import lax
from jax.experimental import pallas as pl
from jax.experimental.pallas import tpu as pltpu
from jax.sharding import PartitionSpec as P

NX, NY = 4, 8
TOPK = 6
CAP = 7
TOK = 32
NC = 4
PAD = 64
ROWS = CAP * NY
SLOTS = NX * PAD
F32, BF16 = jnp.float32, jnp.bfloat16
DOWN, UP = 0, 1


def nn(a, b):
    return jnp.dot(a, b, preferred_element_type=F32)


def nt(a, b):
    return lax.dot_general(a, b, (((1,), (1,)), ((), ())), preferred_element_type=F32)


def iota(shape, axis):
    return lax.broadcasted_iota(jnp.int32, shape, axis)


def wrap(v, n):
    return jnp.where(v >= n, v - n, v)


def halves(v):
    top = v.astype(BF16)
    return top, (v - top.astype(F32)).astype(BF16)


def hops(c, way):
    return 4 if c % 2 == way else 3


def kernel(
    tok_hbm, cot_hbm, routes_f, routes_b, factors_f, factors_b, sg_hbm, su_hbm, wg_hbm, wu_hbm, wd_hbm,
    mixed_hbm, grad_hbm, wgrad_ref,
    wg, wu, wd, sg, su, G, XS, X, OUT, OR, PS, R, SB, OB, MS, MR, SCS, SCR, SYS, SYR,
    S, CH, MT, acc_a, acc_b, co_g, co_u, co_s,
    ag_s, ag_r, xd_s, xd_r, xr_s, xr_r, rs_s, rs_r, mt_s, mt_r, sc_s, sc_r, sy_s, sy_r, ld, own, outs,
):
    me = lax.axis_index("expert")
    y, x = lax.div(me, NX), lax.rem(me, NX)
    depth = tok_hbm.shape[1]
    W = depth // NC

    def at_y(o):
        return {"expert": lax.rem(y + o, NY) * NX + x}

    def at_x(p):
        return {"expert": y * NX + lax.rem(x + p, NX)}

    def cols(c):
        return pl.ds(c * W, W)

    ins = (tok_hbm, cot_hbm)
    results = (mixed_hbm, grad_hbm)
    remote = pltpu.make_async_remote_copy

    def gather_hop(m, c, way, h):
        a, b = (h, h + 1) if way == DOWN else ((NY - h) % NY, NY - 1 - h)
        src = ins[m].at[:, cols(c)] if h == 0 else G.at[m, c, a]
        return remote(src, G.at[m, c, b], ag_s.at[m, c, way, h], ag_r.at[m, c, way, h],
                      device_id=at_y(NY - 1 if way == DOWN else 1))

    def to_expert(m, c, p):
        q = NX - p
        return remote(XS.at[m, c, p - 1, pl.ds(0, ROWS)], X.at[m, c, q, pl.ds(0, ROWS)],
                      xd_s.at[m, c, p - 1], xd_r.at[m, c, q - 1], device_id=at_x(p))

    def from_expert(m, c, q):
        p = NX - q
        return remote(OUT.at[m, c, q - 1, pl.ds(0, ROWS)], OR.at[m, c, p, pl.ds(0, ROWS)],
                      xr_s.at[m, c, q - 1], xr_r.at[m, c, p - 1], device_id=at_x(q))

    def sum_hop(m, c, way, k):
        return remote(SB.at[m, c, way, k - 1], R.at[m, c, way, k - 1], rs_s.at[m, c, way, k - 1],
                      rs_r.at[m, c, way, k - 1], device_id=at_y(NY - 1 if way == DOWN else 1))

    def meta_to(o):
        return remote(MS.at[o], MR.at[NY - o], mt_s.at[o - 1], mt_r.at[NY - o - 1], device_id=at_y(o))

    def score_to(q):
        return remote(SCS, SCR.at[NX - q - 1], sc_s.at[q - 1], sc_r.at[NX - q - 1], device_id=at_x(q))

    def score_back(o):
        return remote(SYS.at[o], SYR.at[NY - o], sy_s.at[o - 1], sy_r.at[NY - o - 1], device_id=at_y(o))

    def own_rows(m, c):
        return pltpu.make_async_copy(ins[m].at[:, cols(c)], G.at[m, c, 0], own.at[m, c])

    def result(m, c):
        return pltpu.make_async_copy(OB.at[m, c], results[m].at[:, cols(c)], outs.at[m, c])

    barrier = pltpu.get_barrier_semaphore()
    for o in range(1, NY):
        pl.semaphore_signal(barrier, inc=1, device_id=at_y(o))
    for p in range(1, NX):
        pl.semaphore_signal(barrier, inc=1, device_id=at_x(p))
    loads = [
        pltpu.make_async_copy(a, b, ld.at[i])
        for i, (a, b) in enumerate(((sg_hbm, sg), (su_hbm, su), (wg_hbm, wg), (wu_hbm, wu), (wd_hbm, wd)))
    ]
    for load in loads[:2]:
        load.start()
    for m in range(2):
        for c in range(NC):
            own_rows(m, c).start()
    for load in loads[2:]:
        load.start()

    lane = iota((NY, 128), 1)
    named = (wrap(y + iota((NY, 128), 0), NY) * NX + wrap(x + lane // TOK, NX)).astype(F32)
    before = (iota((128, 128), 0) // TOK == iota((128, 128), 1) // TOK) & (iota((128, 128), 0) < iota((128, 128), 1))
    before = before.astype(F32).astype(BF16)
    table, chosen = [], []
    for routes, factors in ((routes_f, factors_f), (routes_b, factors_b)):
        ids = jnp.concatenate([routes[...].astype(F32)] * NX, axis=1)
        shares = jnp.concatenate([factors[...]] * NX, axis=1)
        chosen.append(ids)
        has, weight = jnp.zeros((NY, 128), F32), jnp.zeros((NY, 128), F32)
        for k in range(TOPK):
            hit = named == ids[k:k + 1, :]
            has = has + jnp.where(hit, 1.0, 0.0)
            weight = weight + jnp.where(hit, shares[k:k + 1, :], 0.0)
        slot = nn(has.astype(BF16), before)
        table += [jnp.where(has > 0, slot, -1.0), weight]
    for o in range(NY):
        for i, rows in enumerate(table):
            MS[o, i:i + 1, :] = rows[o:o + 1, :]
        MS[o, 4:8, :] = jnp.zeros((4, 128), F32)
    MR[0] = MS[0]

    for m in range(2):
        for c in range(NC):
            for p in range(1, NX):
                X[m, c, p, ROWS:PAD, :] = jnp.zeros((PAD - ROWS, W), BF16)
                OR[m, c, p, ROWS:PAD, :] = jnp.zeros((PAD - ROWS, W), BF16)

    pl.semaphore_wait(barrier, NY - 1 + NX - 1)

    def start_own(m):
        for c in range(NC):
            for way in (DOWN, UP):
                gather_hop(m, c, way, 0).start()

    def pass_on(m, h):
        for c in range(NC):
            for way in (DOWN, UP):
                if h < hops(c, way):
                    gather_hop(m, c, way, h - 1).wait_recv()
                    gather_hop(m, c, way, h).start()

    for o in range(1, NY):
        meta_to(o).start()
    start_own(0)
    pass_on(0, 1)

    loads[0].wait()
    loads[1].wait()
    r, cj = iota((SLOTS, CAP * TOK), 0), iota((SLOTS, CAP * TOK), 1)
    source = wrap(y + r % NY, NY) * NX + wrap(x + r // PAD, NX)
    order = ((r % PAD) // NY == cj // 32) & (source == cj % 32)
    order = order.astype(F32).astype(BF16)
    ff = wd_hbm.shape[0]
    a = nn(order, sg[...].reshape(CAP * 32, ff))
    u = nn(order, su[...].reshape(CAP * 32, ff))
    sig = 1.0 / (1.0 + jnp.exp(-a))
    act = a * sig
    co_g[...] = u * sig * (1.0 + a * (1.0 - sig))
    co_u[...] = act
    co_s[...] = act * u

    pass_on(0, 2)

    for o in range(1, NY):
        meta_to(o).wait_recv()
    r128, l128 = iota((SLOTS, 128), 0), iota((SLOTS, 128), 1)
    place = l128 // TOK == r128 // PAD
    fold = (r128 % TOK == l128 % TOK).astype(F32).astype(BF16)
    block = iota((SLOTS, SLOTS), 0) % NY == iota((SLOTS, SLOTS), 1) // TOK
    back = iota((SLOTS, SLOTS), 1) % NY == iota((SLOTS, SLOTS), 0) // TOK
    for m in range(2):
        slots = jnp.concatenate([MR[o, 2 * m:2 * m + 1, :] for o in range(NY)], axis=0)
        weights = jnp.concatenate([MR[o, 2 * m + 1:2 * m + 2, :] for o in range(NY)], axis=0)
        slots = jnp.broadcast_to(slots[None], (SLOTS // NY, NY, 128)).reshape(SLOTS, 128)
        weights = jnp.broadcast_to(weights[None], (SLOTS // NY, NY, 128)).reshape(SLOTS, 128)
        hit = (slots == ((r128 % PAD) // NY).astype(F32)) & place
        match = jnp.where(hit, 1.0, 0.0).astype(BF16)
        top = jnp.where(hit, weights, 0.0).astype(BF16)
        S[m] = jnp.where(block, nt(match, fold), 0.0).astype(BF16)
        CH[m] = jnp.where(back, nt(fold, top), 0.0).astype(BF16)
        if m == 1:
            MT[...] = match

    pass_on(0, 3)
    start_own(1)

    def send_slots(m, c):
        own_rows(m, c).wait()
        for way in (DOWN, UP):
            gather_hop(m, c, way, hops(c, way) - 1).wait_recv()
        rows = nn(S[m], G[m, c].reshape(NY * TOK, W)).astype(BF16).reshape(NX, PAD, W)
        for p in range(1, NX):
            XS[m, c, p - 1] = rows[p]
        for p in (2, 1, 3):
            to_expert(m, c, p).start()
        X[m, c, 0] = rows[0]

    def arrived(m, c):
        for p in range(1, NX):
            to_expert(m, c, p).wait_recv()
        return X[m, c].reshape(SLOTS, W)

    def give_back(m, c, value):
        value = value.astype(BF16).reshape(NX, PAD, W)
        for q in range(1, NX):
            OUT[m, c, q - 1] = value[q]
        for q in (2, 1, 3):
            from_expert(m, c, q).start()
        OR[m, c, 0] = value[0]

    def forward(c):
        rows = arrived(0, c)
        g, v = nt(rows, wg[:, cols(c)]), nt(rows, wu[:, cols(c)])
        acc_a[...] = g if c == 0 else acc_a[...] + g
        acc_b[...] = v if c == 0 else acc_b[...] + v

    def send_sum(m, c, way, k):
        o = NY - k if way == DOWN else k
        value = PS[m, c, o]
        if k < hops(c, way):
            sum_hop(m, c, way, k + 1).wait_recv()
            value = value + R[m, c, way, k].astype(F32)
        SB[m, c, way, k - 1] = value.astype(BF16)
        sum_hop(m, c, way, k).start()

    def stage(m, c, s):
        if s == 0:
            for p in range(1, NX):
                from_expert(m, c, NX - p).wait_recv()
            rows = OR[m, c].reshape(SLOTS, W)
            PS[m, c] = nn(CH[m], rows).reshape(NY, TOK, W)
        for way in (DOWN, UP):
            if hops(c, way) > s:
                send_sum(m, c, way, hops(c, way) - s)
        if s == 4:
            for way in (DOWN, UP):
                sum_hop(m, c, way, 1).wait_recv()
            OB[m, c] = (PS[m, c, 0] + R[m, c, DOWN, 0].astype(F32) + R[m, c, UP, 0].astype(F32)).astype(BF16)
            result(m, c).start()

    def scores_on():
        mine = iota((NY, PAD), 1) % NY == iota((NY, PAD), 0)
        total = jnp.zeros((NY, 128), F32)
        for p in range(NX):
            if p:
                score_to(NX - p).wait_recv()
            q = (NX - p) % NX
            row = SCS[:, q * PAD:(q + 1) * PAD] if p == 0 else SCR[p - 1, :, q * PAD:(q + 1) * PAD]
            rest = jnp.where(mine, row, 0.0)
            for _ in range(3):
                top, rest2 = rest.astype(BF16), rest - rest.astype(BF16).astype(F32)
                total = total + nn(top, MT[p * PAD:(p + 1) * PAD, :])
                rest = rest2
        for o in range(NY):
            SYS[o] = jnp.broadcast_to(total[o:o + 1, :], (8, 128))
        for o in range(1, NY):
            score_back(o).start()
        SYR[0] = SYS[0]

    def scores_home():
        for o in range(1, NY):
            score_back(o).wait_recv()
        rows = jnp.concatenate([SYR[o, 0:1, :] for o in range(NY)], axis=0)
        for k in range(TOPK):
            v = jnp.sum(jnp.where(named == chosen[1][k:k + 1, :], rows, 0.0), axis=0, keepdims=True)
            v = jnp.broadcast_to(v, (8, 128))
            v = v + pltpu.roll(v, 64, 1)
            v = v + pltpu.roll(v, 32, 1)
            wgrad_ref[k:k + 1, :] = v[0:1, :TOK]

    def backward(c):
        part = nt(arrived(1, c), wd[:, cols(c)])
        acc_a[...] = part if c == 0 else acc_a[...] + part

    def add_up(m, s):
        for c in range(NC):
            stage(m, c, s)

    for c in range(NC):
        send_slots(0, c)
    pass_on(1, 1)
    for load in loads[2:]:
        load.wait()
    forward(0)
    pass_on(1, 2)
    forward(1)
    pass_on(1, 3)
    forward(2)
    forward(3)
    g = acc_a[...]
    hidden = (g / (1.0 + jnp.exp(-g)) * acc_b[...]).astype(BF16)
    for c in range(NC):
        give_back(0, c, nn(hidden, wd[:, cols(c)]))
    for c in range(NC):
        send_slots(1, c)
    add_up(0, 0)
    backward(0)
    backward(1)
    add_up(0, 1)
    backward(2)
    backward(3)
    add_up(0, 2)
    gh = acc_a[...]
    gg, gu = (gh * co_g[...]).astype(BF16), (gh * co_u[...]).astype(BF16)
    top, rest = halves(gh * co_s[...])
    for c in range(NC):
        give_back(1, c, nn(gg, wg[:, cols(c)]) + nn(gu, wu[:, cols(c)]))
        if c == 1:
            add_up(0, 3)
    ones = jnp.ones((NY, ff), BF16)
    score = nt(ones, top) + nt(ones, rest)
    SCS[...] = score
    for q in range(1, NX):
        score_to(q).start()
    add_up(1, 0)
    add_up(0, 4)
    scores_on()
    add_up(1, 1)
    add_up(1, 2)
    scores_home()
    add_up(1, 3)
    add_up(1, 4)

    items = [(m, c) for m in range(2) for c in range(NC)]
    for m, c in items:
        for way in (DOWN, UP):
            for h in range(hops(c, way)):
                gather_hop(m, c, way, h).wait_send()
                sum_hop(m, c, way, h + 1).wait_send()
        for p in range(1, NX):
            to_expert(m, c, p).wait_send()
            from_expert(m, c, p).wait_send()
    for o in range(1, NY):
        meta_to(o).wait_send()
        score_back(o).wait_send()
    for q in range(1, NX):
        score_to(q).wait_send()
    for m, c in items:
        result(m, c).wait()


def window(tokens, cotangent, routes, routes_back, factors, factors_back, saved_gate, saved_up, w_gate, w_up, w_down):
    depth, ff = tokens.shape[1], w_down.shape[0]
    W = depth // NC
    whole = pl.BlockSpec(memory_space=pl.ANY)
    vmem = pl.BlockSpec(memory_space=pltpu.VMEM)
    dma = pltpu.SemaphoreType.DMA
    return pl.pallas_call(
        kernel,
        name="window",
        out_shape=(
            jax.ShapeDtypeStruct((TOK, depth), BF16),
            jax.ShapeDtypeStruct((TOK, depth), BF16),
            jax.ShapeDtypeStruct((TOPK, TOK), F32),
        ),
        in_specs=[whole, whole, vmem, vmem, vmem, vmem, whole, whole, whole, whole, whole],
        out_specs=(whole, whole, vmem),
        scratch_shapes=[
            pltpu.VMEM((ff, depth), BF16),
            pltpu.VMEM((ff, depth), BF16),
            pltpu.VMEM((ff, depth), BF16),
            pltpu.VMEM((CAP, 32, ff), BF16),
            pltpu.VMEM((CAP, 32, ff), BF16),
            pltpu.VMEM((2, NC, NY, TOK, W), BF16),
            pltpu.VMEM((2, NC, NX - 1, PAD, W), BF16),
            pltpu.VMEM((2, NC, NX, PAD, W), BF16),
            pltpu.VMEM((2, NC, NX - 1, PAD, W), BF16),
            pltpu.VMEM((2, NC, NX, PAD, W), BF16),
            pltpu.VMEM((2, NC, NY, TOK, W), F32),
            pltpu.VMEM((2, NC, 2, 4, TOK, W), BF16),
            pltpu.VMEM((2, NC, 2, 4, TOK, W), BF16),
            pltpu.VMEM((2, NC, TOK, W), BF16),
            pltpu.VMEM((NY, 8, 128), F32),
            pltpu.VMEM((NY, 8, 128), F32),
            pltpu.VMEM((8, SLOTS), F32),
            pltpu.VMEM((NX - 1, 8, SLOTS), F32),
            pltpu.VMEM((NY, 8, 128), F32),
            pltpu.VMEM((NY, 8, 128), F32),
            pltpu.VMEM((2, SLOTS, SLOTS), BF16),
            pltpu.VMEM((2, SLOTS, SLOTS), BF16),
            pltpu.VMEM((SLOTS, 128), BF16),
            pltpu.VMEM((SLOTS, ff), F32),
            pltpu.VMEM((SLOTS, ff), F32),
            pltpu.VMEM((SLOTS, ff), F32),
            pltpu.VMEM((SLOTS, ff), F32),
            pltpu.VMEM((SLOTS, ff), F32),
            dma((2, NC, 2, 4)), dma((2, NC, 2, 4)),
            dma((2, NC, 3)), dma((2, NC, 3)),
            dma((2, NC, 3)), dma((2, NC, 3)),
            dma((2, NC, 2, 4)), dma((2, NC, 2, 4)),
            dma((7,)), dma((7,)), dma((3,)), dma((3,)), dma((7,)), dma((7,)),
            dma((5,)), dma((2, NC)), dma((2, NC)),
        ],
        compiler_params=pltpu.CompilerParams(
            collective_id=0, has_side_effects=True, vmem_limit_bytes=60 * 1024 * 1024
        ),
    )(tokens, cotangent, routes, routes_back, factors, factors_back, saved_gate, saved_up, w_gate, w_up, w_down)


def hand_over(a_ref, b_ref, c_ref, a_out, b_out, c_out):
    a_out[...] = a_ref[...]
    b_out[...] = b_ref[...]
    c_out[...] = c_ref[...]


def body(
    tokens, routes, weights_fwd, cotangent, routes_back, weights_back, saved_gate, saved_up, w_gate, w_up, w_down
):
    parts = window(
        tokens, cotangent, routes.T, routes_back.T, weights_fwd.T, weights_back.T,
        saved_gate[0, :, 0].transpose(1, 0, 2), saved_up[0, :, 0].transpose(1, 0, 2),
        w_gate[0].T, w_up[0].T, w_down[0],
    )
    mixed, input_grad, wgrad = pl.pallas_call(
        hand_over, name="hand_over", out_shape=tuple(jax.ShapeDtypeStruct(v.shape, v.dtype) for v in parts)
    )(*parts)
    return mixed, input_grad, wgrad.T


def solution(mesh):
    rows = P(("dp", "expert"), None)
    saved = P("dp", None, "expert", None, None)
    weight = P("expert", None, None)
    return jax.shard_map(
        body,
        mesh=mesh,
        in_specs=(rows,) * 6 + (saved, saved, weight, weight, weight),
        out_specs=(rows, rows, rows),
        check_vma=False,
    )
```

```python
import jax
import jax.numpy as jnp
from jax import lax
from jax.experimental import pallas as pl
from jax.experimental.pallas import tpu as pltpu
from jax.sharding import PartitionSpec as P

NX, NY = 4, 8
TOPK = 6
CAP = 7
TOK = 32
NC = 4
PAD = 64
ROWS = CAP * NY
SLOTS = NX * PAD
F32, BF16 = jnp.float32, jnp.bfloat16
DOWN, UP = 0, 1


def nn(a, b):
    return jnp.dot(a, b, preferred_element_type=F32)


def nt(a, b):
    return lax.dot_general(a, b, (((1,), (1,)), ((), ())), preferred_element_type=F32)


def iota(shape, axis):
    return lax.broadcasted_iota(jnp.int32, shape, axis)


def wrap(v, n):
    return jnp.where(v >= n, v - n, v)


def halves(v):
    top = v.astype(BF16)
    return top, (v - top.astype(F32)).astype(BF16)


def hops(c, way):
    return 4 if c % 2 == way else 3


def kernel(
    tok_hbm, cot_hbm, routes_f, routes_b, factors_f, factors_b, sg_hbm, su_hbm, wg_hbm, wu_hbm, wd_hbm,
    mixed_hbm, grad_hbm, wgrad_ref,
    wg, wu, wd, sg, su, G, XS, X, OUT, OR, PS, R, SB, OB, MS, MR, SCS, SCR, SYS, SYR,
    S, CH, MT, acc_a, acc_b, co_g, co_u, co_s,
    ag_s, ag_r, xd_s, xd_r, xr_s, xr_r, rs_s, rs_r, mt_s, mt_r, sc_s, sc_r, sy_s, sy_r, ld, own, outs,
):
    me = lax.axis_index("expert")
    y, x = lax.div(me, NX), lax.rem(me, NX)
    depth = tok_hbm.shape[1]
    W = depth // NC

    def at_y(o):
        return {"expert": lax.rem(y + o, NY) * NX + x}

    def at_x(p):
        return {"expert": y * NX + lax.rem(x + p, NX)}

    def cols(c):
        return pl.ds(c * W, W)

    ins = (tok_hbm, cot_hbm)
    results = (mixed_hbm, grad_hbm)
    remote = pltpu.make_async_remote_copy

    def gather_hop(m, c, way, h):
        a, b = (h, h + 1) if way == DOWN else ((NY - h) % NY, NY - 1 - h)
        src = ins[m].at[:, cols(c)] if h == 0 else G.at[m, c, a]
        return remote(src, G.at[m, c, b], ag_s.at[m, c, way, h], ag_r.at[m, c, way, h],
                      device_id=at_y(NY - 1 if way == DOWN else 1))

    def to_expert(m, c, p):
        q = NX - p
        return remote(XS.at[m, c, p - 1, pl.ds(0, ROWS)], X.at[m, c, q, pl.ds(0, ROWS)],
                      xd_s.at[m, c, p - 1], xd_r.at[m, c, q - 1], device_id=at_x(p))

    def from_expert(m, c, q):
        p = NX - q
        return remote(OUT.at[m, c, q - 1, pl.ds(0, ROWS)], OR.at[m, c, p, pl.ds(0, ROWS)],
                      xr_s.at[m, c, q - 1], xr_r.at[m, c, p - 1], device_id=at_x(q))

    def sum_hop(m, c, way, k):
        return remote(SB.at[m, c, way, k - 1], R.at[m, c, way, k - 1], rs_s.at[m, c, way, k - 1],
                      rs_r.at[m, c, way, k - 1], device_id=at_y(NY - 1 if way == DOWN else 1))

    def meta_to(o):
        return remote(MS.at[o], MR.at[NY - o], mt_s.at[o - 1], mt_r.at[NY - o - 1], device_id=at_y(o))

    def score_to(q):
        return remote(SCS, SCR.at[NX - q - 1], sc_s.at[q - 1], sc_r.at[NX - q - 1], device_id=at_x(q))

    def score_back(o):
        return remote(SYS.at[o], SYR.at[NY - o], sy_s.at[o - 1], sy_r.at[NY - o - 1], device_id=at_y(o))

    def own_rows(m, c):
        return pltpu.make_async_copy(ins[m].at[:, cols(c)], G.at[m, c, 0], own.at[m, c])

    def result(m, c):
        return pltpu.make_async_copy(OB.at[m, c], results[m].at[:, cols(c)], outs.at[m, c])

    barrier = pltpu.get_barrier_semaphore()
    for o in range(1, NY):
        pl.semaphore_signal(barrier, inc=1, device_id=at_y(o))
    for p in range(1, NX):
        pl.semaphore_signal(barrier, inc=1, device_id=at_x(p))
    loads = [
        pltpu.make_async_copy(a, b, ld.at[i])
        for i, (a, b) in enumerate(((sg_hbm, sg), (su_hbm, su), (wg_hbm, wg), (wu_hbm, wu), (wd_hbm, wd)))
    ]
    for load in loads[:2]:
        load.start()
    for m in range(2):
        for c in range(NC):
            own_rows(m, c).start()
    for load in loads[2:]:
        load.start()

    lane = iota((NY, 128), 1)
    named = (wrap(y + iota((NY, 128), 0), NY) * NX + wrap(x + lane // TOK, NX)).astype(F32)
    before = (iota((128, 128), 0) // TOK == iota((128, 128), 1) // TOK) & (iota((128, 128), 0) < iota((128, 128), 1))
    before = before.astype(F32).astype(BF16)
    table, chosen = [], []
    for routes, factors in ((routes_f, factors_f), (routes_b, factors_b)):
        ids = jnp.concatenate([routes[...].astype(F32)] * NX, axis=1)
        shares = jnp.concatenate([factors[...]] * NX, axis=1)
        chosen.append(ids)
        has, weight = jnp.zeros((NY, 128), F32), jnp.zeros((NY, 128), F32)
        for k in range(TOPK):
            hit = named == ids[k:k + 1, :]
            has = has + jnp.where(hit, 1.0, 0.0)
            weight = weight + jnp.where(hit, shares[k:k + 1, :], 0.0)
        slot = nn(has.astype(BF16), before)
        table += [jnp.where(has > 0, slot, -1.0), weight]
    for o in range(NY):
        for i, rows in enumerate(table):
            MS[o, i:i + 1, :] = rows[o:o + 1, :]
        MS[o, 4:8, :] = jnp.zeros((4, 128), F32)
    MR[0] = MS[0]

    for m in range(2):
        for c in range(NC):
            for p in range(1, NX):
                X[m, c, p, ROWS:PAD, :] = jnp.zeros((PAD - ROWS, W), BF16)
                OR[m, c, p, ROWS:PAD, :] = jnp.zeros((PAD - ROWS, W), BF16)

    pl.semaphore_wait(barrier, NY - 1 + NX - 1)

    def start_own(m):
        for c in range(NC):
            for way in (DOWN, UP):
                gather_hop(m, c, way, 0).start()

    def pass_on(m, h):
        for c in range(NC):
            for way in (DOWN, UP):
                if h < hops(c, way):
                    gather_hop(m, c, way, h - 1).wait_recv()
                    gather_hop(m, c, way, h).start()

    for o in range(1, NY):
        meta_to(o).start()
    start_own(0)
    pass_on(0, 1)

    pass_on(0, 2)

    for o in range(1, NY):
        meta_to(o).wait_recv()
    r128, l128 = iota((SLOTS, 128), 0), iota((SLOTS, 128), 1)
    place = l128 // TOK == r128 // PAD
    fold = (r128 % TOK == l128 % TOK).astype(F32).astype(BF16)
    block = iota((SLOTS, SLOTS), 0) % NY == iota((SLOTS, SLOTS), 1) // TOK
    back = iota((SLOTS, SLOTS), 1) % NY == iota((SLOTS, SLOTS), 0) // TOK

    def tables(m):
        slots = jnp.concatenate([MR[o, 2 * m:2 * m + 1, :] for o in range(NY)], axis=0)
        weights = jnp.concatenate([MR[o, 2 * m + 1:2 * m + 2, :] for o in range(NY)], axis=0)
        slots = jnp.broadcast_to(slots[None], (SLOTS // NY, NY, 128)).reshape(SLOTS, 128)
        weights = jnp.broadcast_to(weights[None], (SLOTS // NY, NY, 128)).reshape(SLOTS, 128)
        hit = (slots == ((r128 % PAD) // NY).astype(F32)) & place
        match = jnp.where(hit, 1.0, 0.0).astype(BF16)
        top = jnp.where(hit, weights, 0.0).astype(BF16)
        S[m] = jnp.where(block, nt(match, fold), 0.0).astype(BF16)
        CH[m] = jnp.where(back, nt(fold, top), 0.0).astype(BF16)
        if m == 1:
            MT[...] = match

    tables(0)
    pass_on(0, 3)
    start_own(1)

    def send_slots(m, c):
        own_rows(m, c).wait()
        for way in (DOWN, UP):
            gather_hop(m, c, way, hops(c, way) - 1).wait_recv()
        rows = nn(S[m], G[m, c].reshape(NY * TOK, W)).astype(BF16).reshape(NX, PAD, W)
        for p in range(1, NX):
            XS[m, c, p - 1] = rows[p]
        for p in (2, 1, 3):
            to_expert(m, c, p).start()
        X[m, c, 0] = rows[0]

    def arrived(m, c):
        for p in range(1, NX):
            to_expert(m, c, p).wait_recv()
        return X[m, c].reshape(SLOTS, W)

    def give_back(m, c, value):
        value = value.astype(BF16).reshape(NX, PAD, W)
        for q in range(1, NX):
            OUT[m, c, q - 1] = value[q]
        for q in (2, 1, 3):
            from_expert(m, c, q).start()
        OR[m, c, 0] = value[0]

    def forward(c):
        rows = arrived(0, c)
        g, v = nt(rows, wg[:, cols(c)]), nt(rows, wu[:, cols(c)])
        acc_a[...] = g if c == 0 else acc_a[...] + g
        acc_b[...] = v if c == 0 else acc_b[...] + v

    def send_sum(m, c, way, k):
        o = NY - k if way == DOWN else k
        value = PS[m, c, o]
        if k < hops(c, way):
            sum_hop(m, c, way, k + 1).wait_recv()
            value = value + R[m, c, way, k].astype(F32)
        SB[m, c, way, k - 1] = value.astype(BF16)
        sum_hop(m, c, way, k).start()

    def stage(m, c, s):
        if s == 0:
            for p in range(1, NX):
                from_expert(m, c, NX - p).wait_recv()
            rows = OR[m, c].reshape(SLOTS, W)
            PS[m, c] = nn(CH[m], rows).reshape(NY, TOK, W)
        for way in (DOWN, UP):
            if hops(c, way) > s:
                send_sum(m, c, way, hops(c, way) - s)
        if s == 4:
            for way in (DOWN, UP):
                sum_hop(m, c, way, 1).wait_recv()
            OB[m, c] = (PS[m, c, 0] + R[m, c, DOWN, 0].astype(F32) + R[m, c, UP, 0].astype(F32)).astype(BF16)
            result(m, c).start()

    def scores_on():
        mine = iota((NY, PAD), 1) % NY == iota((NY, PAD), 0)
        total = jnp.zeros((NY, 128), F32)
        for p in range(NX):
            if p:
                score_to(NX - p).wait_recv()
            q = (NX - p) % NX
            row = SCS[:, q * PAD:(q + 1) * PAD] if p == 0 else SCR[p - 1, :, q * PAD:(q + 1) * PAD]
            rest = jnp.where(mine, row, 0.0)
            for _ in range(3):
                top, rest2 = rest.astype(BF16), rest - rest.astype(BF16).astype(F32)
                total = total + nn(top, MT[p * PAD:(p + 1) * PAD, :])
                rest = rest2
        for o in range(NY):
            SYS[o] = jnp.broadcast_to(total[o:o + 1, :], (8, 128))
        for o in range(1, NY):
            score_back(o).start()
        SYR[0] = SYS[0]

    def scores_home():
        for o in range(1, NY):
            score_back(o).wait_recv()
        rows = jnp.concatenate([SYR[o, 0:1, :] for o in range(NY)], axis=0)
        for k in range(TOPK):
            v = jnp.sum(jnp.where(named == chosen[1][k:k + 1, :], rows, 0.0), axis=0, keepdims=True)
            v = jnp.broadcast_to(v, (8, 128))
            v = v + pltpu.roll(v, 64, 1)
            v = v + pltpu.roll(v, 32, 1)
            wgrad_ref[k:k + 1, :] = v[0:1, :TOK]

    def backward(c):
        part = nt(arrived(1, c), wd[:, cols(c)])
        acc_a[...] = part if c == 0 else acc_a[...] + part

    def add_up(m, s):
        for c in range(NC):
            stage(m, c, s)

    for c in range(NC):
        send_slots(0, c)
    pass_on(1, 1)
    loads[0].wait()
    loads[1].wait()
    r, cj = iota((SLOTS, CAP * TOK), 0), iota((SLOTS, CAP * TOK), 1)
    source = wrap(y + r % NY, NY) * NX + wrap(x + r // PAD, NX)
    order = ((r % PAD) // NY == cj // 32) & (source == cj % 32)
    order = order.astype(F32).astype(BF16)
    ff = wd_hbm.shape[0]
    a = nn(order, sg[...].reshape(CAP * 32, ff))
    u = nn(order, su[...].reshape(CAP * 32, ff))
    sig = 1.0 / (1.0 + jnp.exp(-a))
    act = a * sig
    co_g[...] = u * sig * (1.0 + a * (1.0 - sig))
    co_u[...] = act
    co_s[...] = act * u

    for load in loads[2:]:
        load.wait()
    pass_on(1, 2)
    tables(1)
    forward(0)
    pass_on(1, 3)
    forward(1)
    forward(2)
    forward(3)
    g = acc_a[...]
    hidden = (g / (1.0 + jnp.exp(-g)) * acc_b[...]).astype(BF16)
    for c in range(NC):
        give_back(0, c, nn(hidden, wd[:, cols(c)]))
    for c in range(NC):
        send_slots(1, c)
    add_up(0, 0)
    backward(0)
    backward(1)
    add_up(0, 1)
    backward(2)
    backward(3)
    add_up(0, 2)
    gh = acc_a[...]
    gg, gu = (gh * co_g[...]).astype(BF16), (gh * co_u[...]).astype(BF16)
    top, rest = halves(gh * co_s[...])
    for c in range(NC):
        give_back(1, c, nn(gg, wg[:, cols(c)]) + nn(gu, wu[:, cols(c)]))
        if c == 1:
            add_up(0, 3)
    ones = jnp.ones((NY, ff), BF16)
    score = nt(ones, top) + nt(ones, rest)
    SCS[...] = score
    for q in range(1, NX):
        score_to(q).start()
    add_up(1, 0)
    add_up(0, 4)
    scores_on()
    add_up(1, 1)
    add_up(1, 2)
    scores_home()
    add_up(1, 3)
    add_up(1, 4)

    items = [(m, c) for m in range(2) for c in range(NC)]
    for m, c in items:
        for way in (DOWN, UP):
            for h in range(hops(c, way)):
                gather_hop(m, c, way, h).wait_send()
                sum_hop(m, c, way, h + 1).wait_send()
        for p in range(1, NX):
            to_expert(m, c, p).wait_send()
            from_expert(m, c, p).wait_send()
    for o in range(1, NY):
        meta_to(o).wait_send()
        score_back(o).wait_send()
    for q in range(1, NX):
        score_to(q).wait_send()
    for m, c in items:
        result(m, c).wait()


def window(tokens, cotangent, routes, routes_back, factors, factors_back, saved_gate, saved_up, w_gate, w_up, w_down):
    depth, ff = tokens.shape[1], w_down.shape[0]
    W = depth // NC
    whole = pl.BlockSpec(memory_space=pl.ANY)
    vmem = pl.BlockSpec(memory_space=pltpu.VMEM)
    dma = pltpu.SemaphoreType.DMA
    return pl.pallas_call(
        kernel,
        name="window",
        out_shape=(
            jax.ShapeDtypeStruct((TOK, depth), BF16),
            jax.ShapeDtypeStruct((TOK, depth), BF16),
            jax.ShapeDtypeStruct((TOPK, TOK), F32),
        ),
        in_specs=[whole, whole, vmem, vmem, vmem, vmem, whole, whole, whole, whole, whole],
        out_specs=(whole, whole, vmem),
        scratch_shapes=[
            pltpu.VMEM((ff, depth), BF16),
            pltpu.VMEM((ff, depth), BF16),
            pltpu.VMEM((ff, depth), BF16),
            pltpu.VMEM((CAP, 32, ff), BF16),
            pltpu.VMEM((CAP, 32, ff), BF16),
            pltpu.VMEM((2, NC, NY, TOK, W), BF16),
            pltpu.VMEM((2, NC, NX - 1, PAD, W), BF16),
            pltpu.VMEM((2, NC, NX, PAD, W), BF16),
            pltpu.VMEM((2, NC, NX - 1, PAD, W), BF16),
            pltpu.VMEM((2, NC, NX, PAD, W), BF16),
            pltpu.VMEM((2, NC, NY, TOK, W), F32),
            pltpu.VMEM((2, NC, 2, 4, TOK, W), BF16),
            pltpu.VMEM((2, NC, 2, 4, TOK, W), BF16),
            pltpu.VMEM((2, NC, TOK, W), BF16),
            pltpu.VMEM((NY, 8, 128), F32),
            pltpu.VMEM((NY, 8, 128), F32),
            pltpu.VMEM((8, SLOTS), F32),
            pltpu.VMEM((NX - 1, 8, SLOTS), F32),
            pltpu.VMEM((NY, 8, 128), F32),
            pltpu.VMEM((NY, 8, 128), F32),
            pltpu.VMEM((2, SLOTS, SLOTS), BF16),
            pltpu.VMEM((2, SLOTS, SLOTS), BF16),
            pltpu.VMEM((SLOTS, 128), BF16),
            pltpu.VMEM((SLOTS, ff), F32),
            pltpu.VMEM((SLOTS, ff), F32),
            pltpu.VMEM((SLOTS, ff), F32),
            pltpu.VMEM((SLOTS, ff), F32),
            pltpu.VMEM((SLOTS, ff), F32),
            dma((2, NC, 2, 4)), dma((2, NC, 2, 4)),
            dma((2, NC, 3)), dma((2, NC, 3)),
            dma((2, NC, 3)), dma((2, NC, 3)),
            dma((2, NC, 2, 4)), dma((2, NC, 2, 4)),
            dma((7,)), dma((7,)), dma((3,)), dma((3,)), dma((7,)), dma((7,)),
            dma((5,)), dma((2, NC)), dma((2, NC)),
        ],
        compiler_params=pltpu.CompilerParams(
            collective_id=0, has_side_effects=True, vmem_limit_bytes=60 * 1024 * 1024
        ),
    )(tokens, cotangent, routes, routes_back, factors, factors_back, saved_gate, saved_up, w_gate, w_up, w_down)


def hand_over(a_ref, b_ref, c_ref, a_out, b_out, c_out):
    a_out[...] = a_ref[...]
    b_out[...] = b_ref[...]
    c_out[...] = c_ref[...]


def body(
    tokens, routes, weights_fwd, cotangent, routes_back, weights_back, saved_gate, saved_up, w_gate, w_up, w_down
):
    parts = window(
        tokens, cotangent, routes.T, routes_back.T, weights_fwd.T, weights_back.T,
        saved_gate[0, :, 0].transpose(1, 0, 2), saved_up[0, :, 0].transpose(1, 0, 2),
        w_gate[0].T, w_up[0].T, w_down[0],
    )
    mixed, input_grad, wgrad = pl.pallas_call(
        hand_over, name="hand_over", out_shape=tuple(jax.ShapeDtypeStruct(v.shape, v.dtype) for v in parts)
    )(*parts)
    return mixed, input_grad, wgrad.T


def solution(mesh):
    rows = P(("dp", "expert"), None)
    saved = P("dp", None, "expert", None, None)
    weight = P("expert", None, None)
    return jax.shard_map(
        body,
        mesh=mesh,
        in_specs=(rows,) * 6 + (saved, saved, weight, weight, weight),
        out_specs=(rows, rows, rows),
        check_vma=False,
    )
```
